256 devices in a mesh: grp: 64 (over z, y_lo, x), tp: 4 (over y_hi, core).
Axes of the slice: x: 4, y: 4 (y_hi: 2, y_lo: 2; y = y_hi * 2 + y_lo), z: 8, core: 2. Of those that a mesh axis runs over, the one named last changes fastest.
Arguments:
- prefix_keys: bfloat16 [16, 1024, 1024], P(None, ('grp', 'tp')), may hold values from -4.5 to 4.5
- prefix_values: bfloat16 [16, 1024, 1024], P(None, ('grp', 'tp')), may hold values from -24 to 24
- cand_queries: bfloat16 [64, 4, 256, 8192], P('grp', None, None, 'tp'), may hold values from -120 to 120
- cand_keys: bfloat16 [64, 4, 256, 1024], P('grp', None, None, 'tp'), may hold values from -4.2 to 4.2
- cand_values: bfloat16 [64, 4, 256, 1024], P('grp', None, None, 'tp'), may hold values from -24 to 24
- live_counts: int32 [64], replicated, may hold values from 1 to 4, as said below
- assignment: int32 [64], replicated, may hold values from 0 to 15
Outputs:
- attended: bfloat16 [64, 4, 256, 8192], P('grp', None, None, 'tp')
The draws below stay inside these ranges and needn't reach their ends.
Inputs may be any that keep to these rules, and one draw needn't show every extreme that they name: The live passages of group g fill slots 0 to live_counts[g] - 1; some group has 4, and the group whose index differs from it in the lowest bit has 1.
All inputs are finite; a program needn't handle non-finite values.
Results may differ from the reference program's by a relative error of at most 0.0045.
Values may be sent and summed in bfloat16 or wider, within the bound.
A program may use at most 64 MiB of HBM per device.

```python
import math
import jax
import jax.numpy as jnp
from jax import lax

HEADS = 64
KV_HEADS = 8
HEAD_DIM = 128
QUERIES = 16
PASS = 256
C_MAX = 4
PREFIX = 1024
GROUPS = 64


def drawn_pair(key):
    base = jax.random.fold_in(key, 17)
    key_draw = jax.random.normal(jax.random.fold_in(base, 1), (GROUPS, C_MAX, PASS, KV_HEADS * HEAD_DIM), jnp.float32)
    key_draw = jnp.clip(key_draw, -4.0, 4.0)
    query_draw = 2.0 * jax.random.normal(jax.random.fold_in(base, 2), (GROUPS, C_MAX, PASS, HEADS * HEAD_DIM), jnp.float32)
    query_draw = jnp.clip(query_draw, -8.0, 8.0)
    return (query_draw, key_draw)


def draw_cand_queries(key, part):
    return drawn_pair(key)[0].astype(jnp.bfloat16)


def draw_cand_keys(key, part):
    return drawn_pair(key)[1].astype(jnp.bfloat16)


def draw_live_counts(key, part):
    index = jnp.arange(GROUPS, dtype=jnp.int32)
    selector = jax.random.randint(jax.random.fold_in(key, 5), (GROUPS,), 0, 4, dtype=jnp.int32)
    spread = jax.random.randint(jax.random.fold_in(key, 6), (GROUPS,), 1, C_MAX + 1, dtype=jnp.int32)
    counts = jnp.where(selector == 0, spread, jnp.ones((GROUPS,), jnp.int32))
    busiest = jax.random.randint(jax.random.fold_in(key, 7), (), 0, GROUPS, dtype=jnp.int32)
    counts = jnp.where(index == busiest, jnp.full((GROUPS,), C_MAX, jnp.int32), counts)
    neighbour = jnp.bitwise_xor(busiest, 1)
    counts = jnp.where(index == neighbour, jnp.ones((GROUPS,), jnp.int32), counts)
    return counts.astype(jnp.int32)


def plant(drawn, key, smallest, largest):
    longest = drawn.shape.index(max(drawn.shape))
    spots = []
    for shift in (0, 1):
        where = [jax.random.randint(jax.random.fold_in(key, axis), (), 0, length) for axis, length in enumerate(drawn.shape)]
        where[longest] = (where[longest] + shift) % drawn.shape[longest]
        spots.append(tuple(where))
    return drawn.at[spots[0]].set(smallest).at[spots[1]].set(largest)


def steps_of(rng, shape, pieces, smallest, top_value):
    gain = 1.0
    for position, blocks in pieces:
        draws = jax.random.uniform(jax.random.fold_in(jax.random.fold_in(rng, 6), position), (blocks,), jnp.float32, smallest / len(pieces), top_value / len(pieces))
        gain = gain * jnp.repeat(jnp.exp(draws), shape[position] // blocks).reshape((-1,) + (1,) * (len(shape) - 1 - position))
    return gain


def bell_draw(stream_key, shape, deviation, most, pieces=(), kind=jnp.bfloat16):
    level = steps_of(stream_key, shape, pieces, -0.22, 0.18) if pieces else 1.0
    entries = jax.random.normal(stream_key, shape, jnp.float32) * deviation * level
    return jnp.minimum(jnp.maximum(entries, -most), most).astype(kind)


def setup_inputs(seed: int = 0) -> dict:
    splits = jax.random.split(jax.random.key(seed), 8)
    return {
        "prefix_keys": bell_draw(splits[0], (QUERIES, PREFIX, KV_HEADS * HEAD_DIM), 1.0, 4.5, ((1, 256),)),
        "prefix_values": bell_draw(splits[1], (QUERIES, PREFIX, KV_HEADS * HEAD_DIM), 4.0, 24.0, ((1, 256),)),
        "cand_queries": draw_cand_queries(jax.random.fold_in(splits[7], 71), 0),
        "cand_keys": draw_cand_keys(jax.random.fold_in(splits[7], 71), 0),
        "cand_values": bell_draw(splits[4], (GROUPS, C_MAX, PASS, KV_HEADS * HEAD_DIM), 4.0, 24.0, ((0, 64), (3, 4))),
        "live_counts": draw_live_counts(jax.random.fold_in(splits[7], 71), 0),
        "assignment": plant(jax.random.randint(splits[6], (GROUPS,), 0, QUERIES), jax.random.fold_in(splits[6], 1), 0, QUERIES - 1).astype(jnp.int32),
    }


masked_score = -1e+30

def head_attention(query_rows, keys, values, visible, ratio):
    rows = query_rows.astype(jnp.float32).reshape(query_rows.shape[0], ratio, HEAD_DIM)
    scores = jnp.einsum('prd,kd->rpk', rows, keys.astype(jnp.float32), precision=lax.Precision.HIGHEST)
    scores = scores * (1.0 / math.sqrt(HEAD_DIM))
    scores = jnp.where(visible[None], scores, masked_score)
    peak = lax.optimization_barrier(jnp.max(scores, axis=-1))
    weights = jnp.exp(scores - peak[..., None])
    total = lax.optimization_barrier(jnp.sum(weights, axis=-1))
    rounded = lax.optimization_barrier(weights.astype(jnp.bfloat16)).astype(jnp.float32)
    mixed = jnp.einsum('rpk,kd->prd', rounded, values.astype(jnp.float32), precision=lax.Precision.HIGHEST)
    mixed = mixed / jnp.transpose(total)[:, :, None]
    return mixed.reshape(query_rows.shape[0], ratio * HEAD_DIM)

def reference(prefix_keys, prefix_values, cand_queries, cand_keys, cand_values, live_counts, assignment):
    ratio = HEADS // KV_HEADS
    width = ratio * HEAD_DIM
    key_index = jnp.arange(PREFIX + PASS, dtype=jnp.int32)
    row_index = jnp.arange(PASS, dtype=jnp.int32)
    visible = (key_index[None, :] < PREFIX) | (key_index[None, :] - PREFIX <= row_index[:, None])
    anchor = jnp.zeros((), jnp.int32)

    def one_group(group):
        chosen = assignment[group].astype(jnp.int32)
        front_keys = lax.dynamic_index_in_dim(prefix_keys, chosen, 0, keepdims=False)
        front_values = lax.dynamic_index_in_dim(prefix_values, chosen, 0, keepdims=False)
        queries = lax.dynamic_index_in_dim(cand_queries, group, 0, keepdims=False)
        own_keys = lax.dynamic_index_in_dim(cand_keys, group, 0, keepdims=False)
        own_values = lax.dynamic_index_in_dim(cand_values, group, 0, keepdims=False)

        def one_item(item):
            slot = (item // KV_HEADS).astype(jnp.int32)
            head = (item % KV_HEADS).astype(jnp.int32)
            query_rows = lax.dynamic_slice(queries, (slot, anchor, head * width), (1, PASS, width))[0]
            near_keys = lax.dynamic_slice(own_keys, (slot, anchor, head * HEAD_DIM), (1, PASS, HEAD_DIM))[0]
            near_values = lax.dynamic_slice(own_values, (slot, anchor, head * HEAD_DIM), (1, PASS, HEAD_DIM))[0]
            far_keys = lax.dynamic_slice_in_dim(front_keys, head * HEAD_DIM, HEAD_DIM, 1)
            far_values = lax.dynamic_slice_in_dim(front_values, head * HEAD_DIM, HEAD_DIM, 1)
            keys = jnp.concatenate([far_keys, near_keys], 0)
            values = jnp.concatenate([far_values, near_values], 0)
            return head_attention(query_rows, keys, values, visible, ratio)
        results = lax.map(one_item, jnp.arange(C_MAX * KV_HEADS, dtype=jnp.int32))
        results = results.reshape(C_MAX, KV_HEADS, PASS, width)
        results = jnp.transpose(results, (0, 2, 1, 3)).reshape(C_MAX, PASS, HEADS * HEAD_DIM)
        results = results.astype(jnp.bfloat16)
        alive = jnp.arange(C_MAX, dtype=jnp.int32) < live_counts[group].astype(jnp.int32)
        return jnp.where(alive[:, None, None], results, jnp.zeros_like(results))
    return lax.map(one_group, jnp.arange(GROUPS, dtype=jnp.int32))
```

```python
import functools
import math

import jax
import jax.numpy as jnp
from jax import lax
from jax.experimental import pallas as pl
from jax.experimental.pallas import tpu as pltpu
from jax.sharding import PartitionSpec as P

HEAD_DIM = 128
TO_EXP2 = math.log2(math.e) / math.sqrt(HEAD_DIM)
masked_score = -1e30
ROWS = 128
DEPTH = 8
PLANE = 32
EARLY = 5
MESH = pl.DeviceIdType.MESH


def with_ones(values):
    return jnp.concatenate([values, jnp.ones_like(values)], axis=1)


def attention_kernel(count_ref, q_ref, far_k_ref, far_v_ref, near_k_ref, near_v_ref, out_ref):
    passage = q_ref.shape[1]
    ratio = q_ref.shape[2] // HEAD_DIM
    live = pl.program_id(1) < count_ref[0]
    over_last = (((1,), (1,)), ((), ()))

    @pl.when(live)
    def _():
        far_k, near_k = far_k_ref[...], near_k_ref[0]
        far_v, near_v = with_ones(far_v_ref[...]), with_ones(near_v_ref[0])
        for r in range(ratio):
            for top in range(0, passage, ROWS):
                rows, cols, seen = pl.ds(top, ROWS), pl.ds(r * HEAD_DIM, HEAD_DIM), top + ROWS
                q = q_ref[0, rows, cols]
                far = lax.dot_general(q, far_k, over_last, preferred_element_type=jnp.float32)
                near = lax.dot_general(q, near_k[:seen], over_last, preferred_element_type=jnp.float32)
                row = lax.broadcasted_iota(jnp.int32, near.shape, 0) + top
                col = lax.broadcasted_iota(jnp.int32, near.shape, 1)
                near = jnp.where(col <= row, near, masked_score)
                peak = jnp.maximum(
                    jnp.max(far, -1, keepdims=True), jnp.max(near, -1, keepdims=True)
                )
                far = jnp.exp2((far - peak) * TO_EXP2).astype(jnp.bfloat16)
                near = jnp.exp2((near - peak) * TO_EXP2).astype(jnp.bfloat16)
                mixed = jnp.dot(far, far_v, preferred_element_type=jnp.float32) + jnp.dot(
                    near, near_v[:seen], preferred_element_type=jnp.float32
                )
                out_ref[0, rows, cols] = (mixed[:, :HEAD_DIM] / mixed[:, HEAD_DIM:]).astype(
                    out_ref.dtype
                )

    @pl.when(jnp.logical_not(live))
    def _():
        out_ref[...] = jnp.zeros_like(out_ref)


def attention(count, queries, far_keys, far_values, near_keys, near_values):
    slots, passage, q_width = queries.shape
    kv_local = near_keys.shape[2] // HEAD_DIM
    head_width = q_width // kv_local
    far_len = far_keys.shape[0]
    far_spec = pl.BlockSpec((far_len, HEAD_DIM), lambda h, s, c: (0, h))
    near_spec = pl.BlockSpec((1, passage, HEAD_DIM), lambda h, s, c: (s, 0, h))
    q_spec = pl.BlockSpec((1, passage, head_width), lambda h, s, c: (s, 0, h))
    return pl.pallas_call(
        attention_kernel,
        out_shape=jax.ShapeDtypeStruct(queries.shape, queries.dtype),
        grid_spec=pltpu.PrefetchScalarGridSpec(
            num_scalar_prefetch=1,
            grid=(kv_local, slots),
            in_specs=[q_spec, far_spec, far_spec, near_spec, near_spec],
            out_specs=q_spec,
        ),
        compiler_params=pltpu.CompilerParams(vmem_limit_bytes=60 * 2**20),
    )(count, queries, far_keys, far_values, near_keys, near_values)


def place():
    group, part = lax.axis_index("grp"), lax.axis_index("tp")
    return group // 8, (part // 2) * 2 + (group // 4) % 2, group % 4, part % 2


def plane_peers():
    z, y, x, core = place()
    peers = []
    for j in range(PLANE):
        y2, x2, core2 = (y + j // 8) % 4, (x + (j // 2) % 4) % 4, (core + j % 2) % 2
        peers.append(((y2 % 2) * 4 + x2, (y2 // 2) * 2 + core2))
    return z, peers


def layer_at(z, i):
    half = (i + 1) // 2
    return lax.rem(z + jnp.where(lax.rem(i, 2) == 1, half, DEPTH - half), DEPTH)


def fetch_kernel(
    assignment_ref, keys_ref, values_ref, far_k_ref, far_v_ref, table, outbox, inbox, sent, landed
):
    z, peers = plane_peers()
    barrier = pltpu.get_barrier_semaphore()

    def greet(layer, first):
        for low, part in peers[first:]:
            pl.semaphore_signal(
                barrier, inc=1, device_id=(layer * 8 + low, part), device_id_type=MESH
            )

    greet(z, 1)
    lax.fori_loop(1, DEPTH, lambda i, c: (greet(layer_at(z, i), 0), c)[1], 0)

    def tabulate(query, carry):
        both = jnp.concatenate(
            [keys_ref[query].astype(jnp.float32), values_ref[query].astype(jnp.float32)], axis=0
        )
        for part in range(4):
            first = both[:, 2 * part * HEAD_DIM : (2 * part + 1) * HEAD_DIM]
            second = both[:, (2 * part + 1) * HEAD_DIM : (2 * part + 2) * HEAD_DIM]
            table[query * 4 + part] = jnp.concatenate([first, second], axis=0).astype(jnp.bfloat16)
        return carry

    lax.fori_loop(0, keys_ref.shape[0], tabulate, 0)

    def pick(group, carry):
        query = assignment_ref[group]
        for part in range(4):
            outbox[group * 4 + part] = table[query * 4 + part]
        return carry

    lax.fori_loop(0, 64, pick, 0)
    pl.semaphore_wait(barrier, DEPTH * PLANE - 1)

    def send(layer, i, j, sem):
        group, part = layer * 8 + peers[j][0], peers[j][1]
        pltpu.make_async_remote_copy(
            src_ref=outbox.at[group * 4 + part],
            dst_ref=inbox.at[i * PLANE + j],
            send_sem=sent,
            recv_sem=landed.at[sem],
            device_id=(group, part),
            device_id_type=MESH,
        ).start()

    me = (z * 8 + peers[0][0]) * 4 + peers[0][1]
    pltpu.make_async_copy(outbox.at[me], inbox.at[0], landed.at[0]).start()
    for j in range(1, PLANE):
        send(z, 0, j, 0)

    def send_layer(sem):
        def body(i, carry):
            layer = layer_at(z, i)
            for j in range(PLANE):
                send(layer, i, j, sem)
            return carry

        return body

    lax.fori_loop(1, EARLY, send_layer(0), 0)
    lax.fori_loop(EARLY, DEPTH, send_layer(1), 0)

    def unpack(at, carry):
        for u in range(4):
            pair = at * 8 + 2 * u
            a, b = inbox[pair].astype(jnp.float32), inbox[pair + 1].astype(jnp.float32)
            low = lax.broadcasted_iota(jnp.int32, (8, HEAD_DIM), 0) < 4
            rows = pl.ds(pl.multiple_of(at * 32 + 8 * u, 8), 8)
            for head in range(2):
                a_head, b_head = a[head * 8 : head * 8 + 8], b[head * 8 : head * 8 + 8]
                cols = pl.ds(head * HEAD_DIM, HEAD_DIM)
                far_k_ref[rows, cols] = jnp.where(low, a_head, pltpu.roll(b_head, 4, 0)).astype(
                    jnp.bfloat16
                )
                far_v_ref[rows, cols] = jnp.where(low, pltpu.roll(a_head, 4, 0), b_head).astype(
                    jnp.bfloat16
                )
        return carry

    early = inbox.at[pl.ds(0, EARLY * PLANE)]
    pltpu.make_async_copy(early, early, landed.at[0]).wait()
    lax.fori_loop(0, EARLY * PLANE // 8, unpack, 0)
    late = inbox.at[pl.ds(EARLY * PLANE, (DEPTH - EARLY) * PLANE)]
    pltpu.make_async_copy(late, late, landed.at[1]).wait()
    lax.fori_loop(EARLY * PLANE // 8, DEPTH * PLANE // 8, unpack, 0)
    gone = outbox.at[pl.ds(0, DEPTH * PLANE - 1)]
    pltpu.make_async_copy(gone, gone, sent).wait()


def fetch(assignment, keys, values):
    vmem = pl.BlockSpec(memory_space=pltpu.VMEM)
    far = jax.ShapeDtypeStruct((DEPTH * PLANE * 4, 2 * HEAD_DIM), jnp.bfloat16)
    box = pltpu.VMEM((DEPTH * PLANE, 16, HEAD_DIM), jnp.bfloat16)
    return pl.pallas_call(
        fetch_kernel,
        out_shape=(far, far),
        in_specs=[pl.BlockSpec(memory_space=pltpu.SMEM), vmem, vmem],
        out_specs=(vmem, vmem),
        scratch_shapes=[
            pltpu.VMEM((64, 16, HEAD_DIM), jnp.bfloat16),
            box,
            box,
            pltpu.SemaphoreType.DMA,
            pltpu.SemaphoreType.DMA((2,)),
        ],
        compiler_params=pltpu.CompilerParams(collective_id=0, has_side_effects=True),
    )(assignment, keys, values)


def per_device(
    prefix_keys, prefix_values, cand_queries, cand_keys, cand_values, live_counts, assignment
):
    count = lax.dynamic_slice_in_dim(live_counts, lax.axis_index("grp"), 1)
    far_keys, far_values = fetch(assignment, prefix_keys, prefix_values)
    return attention(
        count, cand_queries[0], far_keys, far_values, cand_keys[0], cand_values[0]
    )[None]


def solution(mesh):
    placed = (
        P(None, ("grp", "tp"), None),
        P(None, ("grp", "tp"), None),
        P("grp", None, None, "tp"),
        P("grp", None, None, "tp"),
        P("grp", None, None, "tp"),
        P(),
        P(),
    )
    return jax.shard_map(
        per_device,
        mesh=mesh,
        in_specs=placed,
        out_specs=P("grp", None, None, "tp"),
        check_vma=False,
    )
```
